32 devices in a mesh: gx: 4 (over y, core), gy: 8 (over z, x).
Axes of the slice: x: 2, y: 2, z: 4, core: 2. Of those that a mesh axis runs over, the one named last changes fastest.
Arguments:
- a_blocks: bfloat16 [768, 7, 256, 256], P(('gx', 'gy'))
- prolong: bfloat16 [768, 256, 128], P(('gx', 'gy'))
- neighbour: int32 [768, 6], P(('gx', 'gy')), may hold values from 0 to 47, as said below
- ghost_send: int32 [4, 8, 8, 3], P('gx', 'gy'), may hold values from 0 to 23
- fine_agg: int32 [768], P(('gx', 'gy')), may hold values from 0 to 63, as said below
- balance: int32 [4, 8, 8], P('gx', 'gy'), may hold values from 0 to 64, as said below
- coarse_cols: int32 [256, 7], P(('gx', 'gy')), may hold values from 0 to 255, as said below
- loads: bfloat16 [256, 128, 256], P(('gx', 'gy')), may hold values from -48 to 48
Outputs:
- coarse: bfloat16 [256, 7, 128, 128], P(('gx', 'gy'))
- smoothed: bfloat16 [256, 128, 256], P(('gx', 'gy'))
The draws below stay inside these ranges and needn't reach their ends.
Inputs may be any that keep to these rules, and one draw needn't show every extreme that they name: `neighbour`: an entry below 24 names a block row of the same device. An entry v >= 24 names slot (v - 24) % 3 of the blocks sent by the device of the same gx row at gy index (v - 24) // 3, never the device itself; every slot so named is named at least once, and the slots named from one peer are the first few of its 3; some device names all 3 slots of some peer. `fine_agg`: the owner is a device of the same gx row. Each aggregate is named by exactly three fine block rows, on three different devices. At most 3 block rows of one device name aggregates of one owner, and this is reached in every draw. Every named slot has a balance entry below 64, and some owner holds 8 aggregates. `balance`: entry 64 marks a slot that no block row names. Every coarse row of a gx row receives exactly one slot, and one owner sends at most one aggregate to each device. At most 3 block rows of one device have their target coarse row on one device, and this is reached in every draw. coarse_cols[g, 0] = g; the other entries name coarse rows of the same device or of a device whose gy index differs by one, in the same gx row.
All inputs are finite; a program needn't handle non-finite values.
Results may differ from the reference program's by a relative error of at most 0.0051.
Values may be sent and summed in bfloat16 or wider, within the bound.
No kernel may reach another device: no remote copies, remote signals or barrier semaphores. Data moves between devices by JAX's collectives and lax.ppermute only.
A program may use at most 128 MiB of HBM per device.

```python
import math
import jax
import jax.numpy as jnp
from jax import lax

BS = 256
CB = 128
LOADS = 256
K = 7
GCAP = 3
SWEEPS = 2
RB = 24
CR = 8
NF = 768
NCR = 256
N_GX = 4
N_GY = 8
DEVICES = 32


def ownership(key):
    total = N_GY * CR
    if N_GY % 3 == 1:
        inverse_three = (2 * N_GY + 1) // 3
    else:
        inverse_three = (N_GY + 1) // 3
    first_count = min(3, CR)

    def one_row(row_key):
        sub_keys = jax.random.split(row_key, 6)
        q_index = jnp.arange(total, dtype=jnp.int32)
        grid_row = q_index // N_GY
        grid_col = q_index % N_GY
        hot_row = jax.random.randint(sub_keys[0], (), 0, CR).astype(jnp.int32)
        valid = (grid_col > 0) & (grid_row != hot_row)
        scores = jax.random.permutation(sub_keys[1], total).astype(jnp.int32)
        scores = jnp.where(valid, scores, -1)
        order = jnp.argsort(-scores, stable=True).astype(jnp.int32)
        rank = jnp.zeros((total,), jnp.int32).at[order].set(q_index)
        cut_inner = valid & (rank < N_GY - CR)
        start_flag = (grid_col == 0) | cut_inner
        segment = (jnp.cumsum(start_flag.astype(jnp.int32)) - 1).astype(jnp.int32)
        segment_start = lax.cummax(jnp.where(start_flag, q_index, 0), axis=0)
        slot_of = (q_index - segment_start).astype(jnp.int32)
        owner_label = jax.random.permutation(sub_keys[2], N_GY).astype(jnp.int32)[segment]
        base = jax.random.randint(sub_keys[3], (), 0, N_GY).astype(jnp.int32)
        first_offsets = (base - inverse_three * jnp.arange(first_count, dtype=jnp.int32)) % N_GY
        shuffled = jax.random.permutation(sub_keys[4], N_GY).astype(jnp.int32)
        taken = jnp.any(shuffled[:, None] == first_offsets[None, :], axis=1).astype(jnp.int32)
        remaining = shuffled[jnp.argsort(taken, stable=True)]
        offsets = jnp.concatenate([first_offsets, remaining[:CR - first_count]]).astype(jnp.int32)
        receiver = ((grid_col + offsets[grid_row]) % N_GY).astype(jnp.int32)
        order_keys = jax.random.split(sub_keys[5], N_GY)
        orders = jax.vmap(lambda one_key: jax.random.permutation(one_key, CR).astype(jnp.int32))(order_keys)
        coarse_index = (receiver * CR + orders[receiver, grid_row]).astype(jnp.int32)
        position = jnp.arange(N_GY * RB, dtype=jnp.int32)
        q_of_position = position // 3
        values = owner_label[q_of_position] * N_GY + slot_of[q_of_position]
        fine_values = values.reshape(RB, N_GY).T
        slot_table = jnp.full((N_GY, N_GY), N_GY * CR, jnp.int32).at[owner_label, slot_of].set(coarse_index)
        return (fine_values.reshape(-1).astype(jnp.int32), slot_table)
    row_keys = jax.random.split(key, N_GX)
    return jax.vmap(one_row)(row_keys)


def draw_fine_agg(key, part):
    fine_values, tables = ownership(jax.random.fold_in(key, 11))
    return fine_values.reshape(-1).astype(jnp.int32)


def draw_balance(key, part):
    fine_values, tables = ownership(jax.random.fold_in(key, 11))
    return tables.astype(jnp.int32)


def draw_neighbour(key, part):
    entries = RB * (K - 1)

    def one_device(device_key, device):
        sub_keys = jax.random.split(device_key, 4)
        self_gy = device % N_GY
        counts = jax.random.randint(sub_keys[0], (N_GY,), 0, GCAP).astype(jnp.int32)
        shuffled = jax.random.permutation(sub_keys[1], N_GY).astype(jnp.int32)
        moved = jnp.argsort((shuffled == self_gy).astype(jnp.int32))
        first_peer = shuffled[moved[0]]
        second_peer = shuffled[moved[1]]
        counts = counts.at[first_peer].set(GCAP).at[second_peer].set(GCAP).at[self_gy].set(0)
        live_slot = (jnp.arange(GCAP, dtype=jnp.int32)[None, :] < counts[:, None]).reshape(-1)
        live_rank = jnp.cumsum(live_slot.astype(jnp.int32)) - 1
        positions = jax.random.permutation(sub_keys[2], entries).astype(jnp.int32)
        values = jax.random.randint(sub_keys[3], (entries,), 0, RB).astype(jnp.int32)
        slot_value = RB + jnp.arange(N_GY * GCAP, dtype=jnp.int32)
        where_to = jnp.where(live_slot, positions[jnp.clip(live_rank, 0, entries - 1)], entries)
        values = values.at[where_to].set(slot_value, mode='drop')
        return values.reshape(RB, K - 1)
    device_keys = jax.random.split(key, DEVICES)
    result = jax.vmap(one_device)(device_keys, jnp.arange(DEVICES, dtype=jnp.int32))
    return result.reshape(NF, K - 1)


def draw_coarse_cols(key, part):
    rows_all = DEVICES * CR
    row_ids = jnp.arange(rows_all, dtype=jnp.int32)
    device = row_ids // CR
    gy_pos = device % N_GY
    sub_keys = jax.random.split(key, 2)
    device_step = jax.random.randint(sub_keys[0], (rows_all, K - 1), -1, 2).astype(jnp.int32)
    near_gy = jnp.clip(gy_pos[:, None] + device_step, 0, N_GY - 1)
    chosen = jax.random.randint(sub_keys[1], (rows_all, K - 1), 0, CR).astype(jnp.int32)
    others = (device[:, None] - gy_pos[:, None] + near_gy) * CR + chosen
    return jnp.concatenate([row_ids[:, None], others], axis=1).astype(jnp.int32)


def draw_a_blocks(key, part):
    coherent = jnp.where(jnp.arange(K) == 0, 2.0, -1.0 / 3.0).astype(jnp.float32)[:, None, None] * jnp.eye(BS, dtype=jnp.float32)[None]
    noise_scale = 1.0 / math.sqrt(BS)

    def one_row(row_index):
        row_key = jax.random.fold_in(key, row_index)
        sub_keys = jax.random.split(row_key, 2)
        noise_part = jax.random.normal(sub_keys[0], (K, BS, BS), jnp.float32)
        spread = jnp.exp(jax.random.uniform(sub_keys[1], (), jnp.float32, 0.0, math.log(10.0)))
        rise_factor = 1.0 + 2.0 * row_index.astype(jnp.float32) / (NF - 1)
        row_scale = spread * rise_factor / 32.0
        return ((coherent + noise_part * noise_scale) * row_scale).astype(jnp.bfloat16)
    return lax.map(one_row, jnp.arange(NF, dtype=jnp.int32))


def draw_prolong(key, part):
    noise_part = jax.random.normal(key, (NF, BS, CB), jnp.float32)
    identity = jnp.eye(BS, CB, dtype=jnp.float32)
    return (noise_part / math.sqrt(BS) + identity[None]).astype(jnp.bfloat16)


def set_ends(drawn, stream_key, least, high):
    place = [jax.random.randint(jax.random.fold_in(stream_key, axis), (), 0, length) for axis, length in enumerate(drawn.shape)]
    main_axis = drawn.shape.index(max(drawn.shape))
    beside = place[:main_axis] + [(place[main_axis] + 1) % drawn.shape[main_axis]] + place[main_axis + 1:]
    return drawn.at[tuple(place)].set(least).at[tuple(beside)].set(high)


def steps_of(stream_key, dims, shards, least, high):
    gain, own = 1.0, jax.random.fold_in(stream_key, 6)
    for dim, shards_of in shards:
        draws = jnp.exp(jax.random.uniform(jax.random.fold_in(own, dim), (shards_of,), jnp.float32, least / len(shards), high / len(shards)))
        gain = gain * jnp.repeat(draws, dims[dim] // shards_of).reshape([-1 if axis == dim else 1 for axis in range(len(dims))])
    return gain


def gaussian(stream_key, shape, width, most, shards=(), held_as=jnp.bfloat16):
    array = jax.random.normal(stream_key, shape, jnp.float32) * width
    if len(shards) > 0:
        array = steps_of(stream_key, shape, shards, -0.22, 0.18) * array
    return jnp.clip(array, min=-most, max=most).astype(held_as)


def setup_inputs(seed: int = 0) -> dict:
    key_of = jax.random.split(jax.random.key(seed), 9)
    return {
        "a_blocks": draw_a_blocks(jax.random.fold_in(key_of[8], 71), 0),
        "prolong": draw_prolong(jax.random.fold_in(key_of[8], 71), 0),
        "neighbour": draw_neighbour(jax.random.fold_in(key_of[8], 71), 0),
        "ghost_send": set_ends(jax.random.randint(key_of[3], (N_GX, N_GY, N_GY, GCAP), 0, RB), jax.random.fold_in(key_of[3], 1), 0, RB - 1).astype(jnp.int32),
        "fine_agg": draw_fine_agg(jax.random.fold_in(key_of[8], 71), 0),
        "balance": draw_balance(jax.random.fold_in(key_of[8], 71), 0),
        "coarse_cols": draw_coarse_cols(jax.random.fold_in(key_of[8], 71), 0),
        "loads": gaussian(key_of[7], (NCR, CB, LOADS), 8.0, 48.0, ((0, 32),)),
    }


def reference(a_blocks, prolong, neighbour, ghost_send, fine_agg, balance, coarse_cols, loads):
    group_size = N_GY
    total_rows = a_blocks.shape[0]
    device_of = jnp.arange(total_rows, dtype=jnp.int32) // RB
    gx_of = device_of // group_size
    gy_of = device_of % group_size
    remote = neighbour - RB
    peer_index = jnp.clip(remote // GCAP, 0, group_size - 1).astype(jnp.int32)
    cap_index = jnp.clip(remote % GCAP, 0, GCAP - 1).astype(jnp.int32)
    sent_block = ghost_send[gx_of[:, None], peer_index, gy_of[:, None], cap_index]
    remote_row = (gx_of[:, None] * group_size + peer_index) * RB + sent_block
    local_row = device_of[:, None] * RB + neighbour
    column_rows = jnp.where(neighbour < RB, local_row, remote_row).astype(jnp.int32)
    columns = jnp.concatenate([jnp.arange(total_rows, dtype=jnp.int32)[:, None], column_rows], axis=1)

    def one_row(row_inputs):
        blocks, left_block, column_ids = row_inputs
        right_blocks = prolong[column_ids]
        applied = jnp.einsum("kab,kbc->kac", blocks.astype(jnp.float32), right_blocks.astype(jnp.float32),
                             precision=lax.Precision.HIGHEST).astype(jnp.bfloat16)
        return jnp.einsum("ac,kad->kcd", left_block.astype(jnp.float32), applied.astype(jnp.float32),
                          precision=lax.Precision.HIGHEST).astype(jnp.bfloat16)

    partial_value = lax.map(one_row, (a_blocks, prolong, columns))
    slot_count = balance.shape[2]
    flat_balance = balance.reshape(-1)
    key_index = gx_of * (group_size * slot_count) + fine_agg
    target = (gx_of * (group_size * CR) + flat_balance[key_index]).astype(jnp.int32)
    coarse_rows = loads.shape[0]
    summed = jax.ops.segment_sum(partial_value.astype(jnp.float32), target, num_segments=coarse_rows)
    coarse = summed.astype(jnp.bfloat16)

    magnitude = jnp.sum(jnp.abs(coarse.astype(jnp.float32)), axis=(1, 3))
    largest = jnp.max(magnitude)
    lower_end = largest / 30.0
    centre = (largest + lower_end) / 2.0
    half_width = (largest - lower_end) / 2.0
    sigma_ratio = centre / half_width
    right_side = loads.astype(jnp.float32)
    solution = right_side / centre
    update = solution
    weight_now = 1.0 / sigma_ratio
    for sweep_index in range(SWEEPS):
        rounded = solution.astype(jnp.bfloat16)
        accumulated = jnp.zeros(right_side.shape, jnp.float32)
        for column_slot in range(K):
            picked = rounded[coarse_cols[:, column_slot]]
            accumulated = accumulated + jnp.einsum(
                "gab,gbl->gal", coarse[:, column_slot].astype(jnp.float32), picked.astype(jnp.float32),
                precision=lax.Precision.HIGHEST)
        residual = right_side - accumulated
        weight_next = 1.0 / (2.0 * sigma_ratio - weight_now)
        update = weight_next * weight_now * update + (2.0 * weight_next / half_width) * residual
        solution = solution + update
        weight_now = weight_next
    return coarse, solution.astype(jnp.bfloat16)
```

```python
import functools

import jax
import jax.numpy as jnp
from jax import lax
from jax.experimental import pallas as pl
from jax.experimental.pallas import tpu as pltpu
from jax.sharding import PartitionSpec as P

OCAP = 3
MEMBERS = 3
CHUNKS = 3

F32 = jnp.float32
BF16 = jnp.bfloat16
VMEM = pltpu.VMEM
ANY = pl.ANY


def chunks_of(count):
    rest = list(range(1, count))
    parts = CHUNKS - 1
    size = -(-len(rest) // parts)
    return [(0, 1)] + [
        (rest[at], min(size, len(rest) - at)) for at in range(0, len(rest), size)
    ]


def dot(a, b):
    return lax.dot_general(a, b, (((1,), (0,)), ((), ())), preferred_element_type=F32)


def dot_t(a, b):
    return lax.dot_general(a, b, (((0,), (0,)), ((), ())), preferred_element_type=F32)


def galerkin_kernel(first, count, per_step, block_rows, ghosts, order, cols, *refs):
    blocks = refs[: per_step * count]
    prolong = refs[per_step * count]
    arrived = refs[per_step * count + 1] if ghosts else None
    out = refs[-1]
    step = pl.program_id(0)
    for s in range(per_step):
        row = order[step * per_step + s]
        left = prolong[row]
        applied = []
        for k in range(count):
            if first + k == 0:
                right = left
            else:
                col = cols[row, first + k]
                near = prolong[jnp.minimum(col, block_rows - 1)]
                far = arrived[jnp.clip(col - block_rows, 0, ghosts - 1)]
                right = jnp.where(col < block_rows, near, far)
            applied.append(dot(blocks[s * count + k][...], right).astype(BF16))
        width = applied[0].shape[1]
        for k in range(0, count, 2):
            if k + 1 < count:
                both = dot_t(left, jnp.concatenate(applied[k : k + 2], axis=1)).astype(BF16)
                out[s, k] = both[:, :width]
                out[s, k + 1] = both[:, width:]
            else:
                out[s, k] = dot_t(left, applied[k]).astype(BF16)


def galerkin(a_blocks, prolong, arrived, order, cols, first, count):
    rows, _, size, _ = a_blocks.shape
    width = prolong.shape[2]
    slots = order.shape[0]
    per_step = OCAP

    def block_spec(s, k):
        return pl.BlockSpec(
            (None, None, size, size),
            lambda step, order, cols: (order[step * per_step + s], k, 0, 0),
        )

    def whole(array):
        return pl.BlockSpec(array.shape, lambda step, order, cols: (0,) * array.ndim)

    ghosts = 0 if arrived is None else arrived.shape[0]
    pools = [prolong] if arrived is None else [prolong, arrived]
    specs = [block_spec(s, first + k) for s in range(per_step) for k in range(count)]
    return pl.pallas_call(
        functools.partial(galerkin_kernel, first, count, per_step, rows, ghosts),
        out_shape=jax.ShapeDtypeStruct((slots, count, width, width), BF16),
        grid_spec=pltpu.PrefetchScalarGridSpec(
            num_scalar_prefetch=2,
            grid=(slots // per_step,),
            in_specs=specs + [whole(array) for array in pools],
            out_specs=pl.BlockSpec(
                (per_step, count, width, width), lambda step, order, cols: (step, 0, 0, 0)
            ),
        ),
        cost_estimate=pl.CostEstimate(
            flops=2 * slots * count * (size * size * width + size * width * width),
            bytes_accessed=2 * slots * count * (size * size + width * width),
            transcendentals=0,
        ),
        name=f"galerkin_{first}",
    )(order, cols, *([a_blocks] * len(specs)), *pools)


def member_sum(members, recv, row, k):
    total = recv[members[row, 0], k].astype(F32)
    for m in range(1, MEMBERS):
        total = total + recv[members[row, m], k].astype(F32)
    return total.astype(BF16)


def gather_kernel(first, count, members, recv, *refs):
    out, held, sem = refs[-3:]
    rows = held.shape[0]

    def one(row, carry):
        for k in range(count):
            held[row, k] = member_sum(members, recv, row, k)
        return carry

    lax.fori_loop(0, rows, one, 0)
    copy = pltpu.make_async_copy(held, out.at[:, pl.ds(first, count)], sem)
    copy.start()
    copy.wait()


def gather_rows(members, recv, so_far, shape, first, count):
    rows, _, width, _ = shape
    inputs = [recv] if so_far is None else [recv, so_far]
    return pl.pallas_call(
        functools.partial(gather_kernel, first, count),
        out_shape=jax.ShapeDtypeStruct(shape, BF16),
        grid_spec=pltpu.PrefetchScalarGridSpec(
            num_scalar_prefetch=1,
            in_specs=[pl.BlockSpec(memory_space=VMEM)]
            + ([] if so_far is None else [pl.BlockSpec(memory_space=ANY)]),
            out_specs=pl.BlockSpec(memory_space=ANY),
            scratch_shapes=[VMEM((rows, count, width, width), BF16), pltpu.SemaphoreType.DMA],
        ),
        input_output_aliases={} if so_far is None else {2: 0},
        cost_estimate=pl.CostEstimate(
            flops=2 * recv.size, bytes_accessed=3 * recv.size, transcendentals=0
        ),
        name=f"gather_{first}",
    )(members, *inputs)


def block_row_product(coarse, pool, cols, row, count):
    total = None
    for k in range(0, count, 2):
        if k + 1 < count:
            lhs = jnp.concatenate([coarse[row, k], coarse[row, k + 1]], axis=1)
            rhs = jnp.concatenate([pool[cols[row, k]], pool[cols[row, k + 1]]], axis=0)
        else:
            lhs, rhs = coarse[row, k], pool[cols[row, k]]
        term = dot(lhs, rhs)
        total = term if total is None else total + term
    return total


def first_kernel(
    first, count, blocks, members, cols, recv, so_far, low, own, high,
    out, product, sent, peak, held, pool, row_sums, sem_in, sem_out,
):
    rows = product.shape[0]
    load = pltpu.make_async_copy(so_far.at[:, pl.ds(0, first)], held.at[:, pl.ds(0, first)], sem_in)
    load.start()

    def last(row, carry):
        for k in range(count):
            held[row, first + k] = member_sum(members, recv, row, k)
        return carry

    lax.fori_loop(0, rows, last, 0)
    store = pltpu.make_async_copy(
        held.at[:, pl.ds(first, count)], out.at[:, pl.ds(first, count)], sem_out
    )
    store.start()
    load.wait()

    def sums(row, carry):
        total = jnp.abs(held[row, 0].astype(F32))
        for k in range(1, blocks):
            total = total + jnp.abs(held[row, k].astype(F32))
        return jnp.maximum(carry, jnp.sum(total, axis=1, keepdims=True))

    width = held.shape[2]
    most = lax.fori_loop(0, rows, sums, jnp.zeros((width, 1), F32))
    most = jnp.max(most, axis=0, keepdims=True)
    peak[...] = jnp.broadcast_to(most[None], peak.shape)
    scale = 1.0 / jnp.clip(most, 2.0**-100, 2.0**120)
    for part, source in enumerate((low, own, high)):

        def scaled(row, carry):
            pool[part * rows + row] = (source[row].astype(F32) * scale).astype(BF16)
            return carry

        lax.fori_loop(0, rows, scaled, 0)

    def multiply(row, carry):
        total = block_row_product(held, pool, cols, row, blocks)
        product[row] = total
        sent[row] = total.astype(BF16)
        return carry

    lax.fori_loop(0, rows, multiply, 0)
    store.wait()


def first_product(members, cols, recv, so_far, low, own, high, first, count, devices):
    rows, blocks, width, _ = so_far.shape
    columns = own.shape[2]
    vmem = pl.BlockSpec(memory_space=VMEM)
    hbm = pl.BlockSpec(memory_space=ANY)
    return pl.pallas_call(
        functools.partial(first_kernel, first, count, blocks),
        out_shape=(
            jax.ShapeDtypeStruct(so_far.shape, BF16),
            jax.ShapeDtypeStruct(own.shape, F32),
            jax.ShapeDtypeStruct(own.shape, BF16),
            jax.ShapeDtypeStruct((devices, 8, 128), F32),
        ),
        grid_spec=pltpu.PrefetchScalarGridSpec(
            num_scalar_prefetch=2,
            in_specs=[vmem, hbm, vmem, vmem, vmem],
            out_specs=(hbm, vmem, vmem, vmem),
            scratch_shapes=[
                VMEM(so_far.shape, BF16),
                VMEM((3 * rows, width, columns), BF16),
                VMEM((8, 128), F32),
                pltpu.SemaphoreType.DMA,
                pltpu.SemaphoreType.DMA,
            ],
        ),
        input_output_aliases={3: 0},
        cost_estimate=pl.CostEstimate(
            flops=2 * so_far.size * columns, bytes_accessed=6 * so_far.size, transcendentals=0
        ),
        name="first_product",
    )(members, cols, recv, so_far, low, own, high)


def second_kernel(blocks, cols, near, coarse, low, own, high, product, below, above, peaks, out, pool):
    rows = out.shape[0]
    largest = jnp.max(jnp.max(peaks[...], axis=0)[0:1], axis=1, keepdims=True)
    lower_end = largest / 30.0
    centre = (largest + lower_end) / 2.0
    half_width = (largest - lower_end) / 2.0
    sigma = centre / half_width
    weight_0 = 1.0 / sigma
    weight_1 = 1.0 / (2.0 * sigma - weight_0)
    weight_2 = 1.0 / (2.0 * sigma - weight_1)
    start = 1.0 / centre
    gain_1 = 2.0 * weight_1 / half_width
    gain_2 = 2.0 * weight_2 / half_width
    change = weight_1 * weight_0 * start + gain_1

    def back(slot):
        peak = peaks[near[slot]][0:1, 0:1]
        return gain_1 * (jnp.clip(peak, 2.0**-100, 2.0**120) / centre)

    for part, (source, seen) in enumerate(((low, below), (own, product), (high, above))):
        factor = back(part)

        def iterate(row, carry):
            value = (start + change) * source[row].astype(F32) - factor * seen[row].astype(F32)
            pool[part * rows + row] = value.astype(BF16)
            return carry

        lax.fori_loop(0, rows, iterate, 0)
    mine = back(1)

    def multiply(row, carry):
        right = own[row].astype(F32)
        update = change * right - mine * product[row]
        residual = right - block_row_product(coarse, pool, cols, row, blocks)
        value = start * right + update + (weight_2 * weight_1 * update + gain_2 * residual)
        out[row] = value.astype(BF16)
        return carry

    lax.fori_loop(0, rows, multiply, 0)


def second_product(cols, near, coarse, low, own, high, product, below, above, peaks):
    rows, blocks, width, _ = coarse.shape
    columns = own.shape[2]
    vmem = pl.BlockSpec(memory_space=VMEM)
    return pl.pallas_call(
        functools.partial(second_kernel, blocks),
        out_shape=jax.ShapeDtypeStruct(own.shape, BF16),
        grid_spec=pltpu.PrefetchScalarGridSpec(
            num_scalar_prefetch=2,
            in_specs=[vmem] * 8,
            out_specs=vmem,
            scratch_shapes=[VMEM((3 * rows, width, columns), BF16)],
        ),
        cost_estimate=pl.CostEstimate(
            flops=2 * coarse.size * columns, bytes_accessed=6 * coarse.size, transcendentals=0
        ),
        name="second_product",
    )(cols, near, coarse, low, own, high, product, below, above, peaks)


def exchange(block, axis):
    return lax.all_to_all(block, axis, split_axis=0, concat_axis=0, tiled=True)


def both_ways(block, axis):
    count = lax.axis_size(axis)
    forward = [(i, i + 1) for i in range(count - 1)]
    backward = [(i + 1, i) for i in range(count - 1)]
    return lax.ppermute(block, axis, forward), lax.ppermute(block, axis, backward)


def routes(fine_agg, balance, coarse_rows):
    group = lax.axis_size("gy")
    me = lax.axis_index("gy")
    rows = fine_agg.shape[0]
    facts = jnp.concatenate([fine_agg, balance.reshape(-1)])
    facts = exchange(jnp.broadcast_to(facts[None], (group,) + facts.shape), "gy")
    named, table = facts[:, :rows], facts[:, rows:].reshape(-1)
    keys = jnp.arange(table.shape[0], dtype=jnp.int32)
    target = jnp.sum(
        jnp.where(named[:, :, None] == keys[None, None, :], table[None, None, :], 0), axis=2
    )
    device = target // coarse_rows
    before = jnp.arange(rows)[:, None] > jnp.arange(rows)[None, :]
    rank = jnp.sum(
        ((device[:, :, None] == device[:, None, :]) & before[None]).astype(jnp.int32), axis=2
    )
    mine = (jnp.arange(group) == me)[:, None]
    place = jnp.sum(jnp.where(mine, device * OCAP + rank, 0), axis=0)
    slots = jnp.arange(group * OCAP, dtype=jnp.int32)
    order = jnp.sum(
        jnp.where(place[None, :] == slots[:, None], jnp.arange(rows, dtype=jnp.int32)[None, :], 0),
        axis=1,
    )
    goal = me * coarse_rows + jnp.arange(coarse_rows, dtype=jnp.int32)
    hit = target[None] == goal[:, None, None]
    slot = jnp.arange(group, dtype=jnp.int32)[:, None] * OCAP + rank
    source = jnp.sum(jnp.where(hit, slot[None] + 1, 0), axis=2)
    found = (source > 0).astype(jnp.int32)
    earlier = jnp.arange(group)[:, None] < jnp.arange(group)[None, :]
    ordinal = jnp.sum(found[:, :, None] * earlier[None].astype(jnp.int32), axis=1)
    members = jnp.stack(
        [
            jnp.sum(jnp.where((ordinal == m) & (found > 0), source - 1, 0), axis=1)
            for m in range(MEMBERS)
        ],
        axis=1,
    )
    return order.astype(jnp.int32), members.astype(jnp.int32)


def per_device(a_blocks, prolong, neighbour, ghost_send, fine_agg, balance, coarse_cols, loads):
    block_rows, blocks = a_blocks.shape[:2]
    group = lax.axis_size("gy")
    row_gy = lax.axis_index("gy")
    row_gx = lax.axis_index("gx")
    devices = group * lax.axis_size("gx")
    coarse_rows = loads.shape[0]
    width = prolong.shape[2]

    low, high = both_ways(loads, "gy")
    outgoing = prolong[ghost_send.reshape(-1)]
    arrived = exchange(outgoing, "gy")
    order, members = routes(fine_agg, balance, coarse_rows)
    columns = jnp.concatenate(
        [jnp.arange(block_rows, dtype=jnp.int32)[:, None], neighbour], axis=1
    )
    parts = chunks_of(blocks)
    received = []
    for first, count in parts:
        sent = galerkin(
            a_blocks, prolong, None if first == 0 else arrived, order, columns, first, count
        )
        received.append(exchange(sent, "gy"))
    so_far = None
    for (first, count), recv in zip(parts[:-1], received[:-1]):
        so_far = gather_rows(
            members, recv, so_far, (coarse_rows, blocks, width, width), first, count
        )
    first_col = (row_gx * group + row_gy - 1) * coarse_rows
    local_cols = coarse_cols - first_col
    coarse, product, sent, peak = first_product(
        members, local_cols, received[-1], so_far, low, loads, high, *parts[-1], devices
    )
    below, above = both_ways(sent, "gy")
    peaks = exchange(peak, ("gx", "gy"))
    here = row_gx * group + row_gy
    near = jnp.stack([jnp.maximum(here - 1, 0), here, jnp.minimum(here + 1, devices - 1)])
    smoothed = second_product(
        local_cols, near.astype(jnp.int32), coarse, low, loads, high, product, below, above, peaks
    )
    return coarse, smoothed


def solution(mesh):
    return jax.shard_map(
        per_device,
        mesh=mesh,
        in_specs=(
            P(("gx", "gy"), None, None, None),
            P(("gx", "gy"), None, None),
            P(("gx", "gy"), None),
            P("gx", "gy", None, None),
            P(("gx", "gy")),
            P("gx", "gy", None),
            P(("gx", "gy"), None),
            P(("gx", "gy"), None, None),
        ),
        out_specs=(P(("gx", "gy"), None, None, None), P(("gx", "gy"), None, None)),
        check_vma=False,
    )
```

```python
import functools

import jax
import jax.numpy as jnp
from jax import lax
from jax.experimental import pallas as pl
from jax.experimental.pallas import tpu as pltpu
from jax.sharding import PartitionSpec as P

OCAP = 3
MEMBERS = 3
CHUNKS = (1, 3, 2, 1)

F32 = jnp.float32
BF16 = jnp.bfloat16
VMEM = pltpu.VMEM
ANY = pl.ANY


LIMIT = pltpu.CompilerParams(vmem_limit_bytes=24 << 20)
WIDE = pltpu.CompilerParams(vmem_limit_bytes=46 << 20)


def chunks_of(count):
    parts, at = [], 0
    for size in CHUNKS[:-1]:
        size = min(size, count - at - 1)
        if size > 0:
            parts.append((at, size))
            at += size
    return parts + [(at, count - at)]


def dot(a, b):
    return lax.dot_general(a, b, (((1,), (0,)), ((), ())), preferred_element_type=F32)


def dot_t(a, b):
    return lax.dot_general(a, b, (((0,), (0,)), ((), ())), preferred_element_type=F32)


def pick_kernel(group, cap, me, wanted, prolong, *outs):
    for offset in range(1, group):
        peer = lax.rem(me[0] + offset, group)
        for c in range(cap):
            outs[offset - 1][c] = prolong[wanted[peer, c]]


def pick_ghosts(me, wanted, prolong):
    group, cap = wanted.shape
    shape = jax.ShapeDtypeStruct((cap,) + prolong.shape[1:], BF16)
    vmem = pl.BlockSpec(memory_space=VMEM)
    return pl.pallas_call(
        functools.partial(pick_kernel, group, cap),
        out_shape=[shape] * (group - 1),
        grid_spec=pltpu.PrefetchScalarGridSpec(
            num_scalar_prefetch=2, in_specs=[vmem], out_specs=[vmem] * (group - 1)
        ),
        compiler_params=LIMIT,
        cost_estimate=pl.CostEstimate(
            flops=0, bytes_accessed=4 * prolong.size, transcendentals=0
        ),
        name="pick_ghosts",
    )(me, wanted, prolong)


def fill(sources, pool, sem, at=0):
    copies = []
    for source in sources:
        size = source.shape[0]
        copies.append(pltpu.make_async_copy(source, pool.at[pl.ds(at, size)], sem.at[len(copies)]))
        at += size
    for copy in copies:
        copy.start()
    return copies


def galerkin_kernel(first, count, group, given, order, cols, *refs):
    blocks, refs = refs[: OCAP * count], refs[OCAP * count :]
    pool, sem = refs[-2:]
    outs, sources = refs[-2 - group : -2], refs[:given]
    step = pl.program_id(0)

    @pl.when(step == 0)
    def load():
        for copy in fill(sources, pool, sem):
            copy.wait()

    for s in range(OCAP):
        row = order[step * OCAP + s]
        left = pool[row]
        applied = [
            dot(blocks[s * count + k][...], pool[cols[row, first + k]]).astype(BF16)
            for k in range(count)
        ]
        width = left.shape[1]
        results = []
        for k in range(0, count, 2):
            if k + 1 < count:
                both = dot_t(left, jnp.concatenate(applied[k : k + 2], axis=1)).astype(BF16)
                results += [both[:, :width], both[:, width:]]
            else:
                results.append(dot_t(left, applied[k]).astype(BF16))
        for offset in range(group):

            @pl.when(step == offset)
            def keep():
                for k in range(count):
                    outs[offset][s, k] = results[k]


def galerkin(a_blocks, sources, after, order, cols, first, count):
    _, _, size, _ = a_blocks.shape
    width = sources[0].shape[2]
    slots = order.shape[0]
    group = slots // OCAP

    def block_spec(s, k):
        return pl.BlockSpec(
            (None, None, size, size),
            lambda step, order, cols: (order[step * OCAP + s], k, 0, 0),
        )

    specs = [block_spec(s, first + k) for s in range(OCAP) for k in range(count)]
    out = jax.ShapeDtypeStruct((OCAP, count, width, width), BF16)
    out_spec = pl.BlockSpec(out.shape, lambda step, order, cols: (0, 0, 0, 0))
    held = sum(source.shape[0] for source in sources)
    return pl.pallas_call(
        functools.partial(galerkin_kernel, first, count, group, len(sources)),
        out_shape=[out] * group,
        grid_spec=pltpu.PrefetchScalarGridSpec(
            num_scalar_prefetch=2,
            grid=(group,),
            in_specs=specs + [pl.BlockSpec(memory_space=ANY)] * (len(sources) + len(after)),
            out_specs=[out_spec] * group,
            scratch_shapes=[
                VMEM((held, size, width), BF16),
                pltpu.SemaphoreType.DMA((len(sources),)),
            ],
        ),
        compiler_params=WIDE,
        cost_estimate=pl.CostEstimate(
            flops=2 * slots * count * (size * size * width + size * width * width),
            bytes_accessed=2 * slots * count * (size * size + width * width),
            transcendentals=0,
        ),
        name=f"galerkin_{first}",
    )(order, cols, *([a_blocks] * len(specs)), *sources, *after)


def member_sum(members, pool, row, k):
    total = pool[members[row, 0], k].astype(F32)
    for m in range(1, MEMBERS):
        total = total + pool[members[row, m], k].astype(F32)
    return total.astype(BF16)


def gather_kernel(first, count, sources, members, *refs):
    out, pool, held, sem, sem_out = refs[-5:]
    for copy in fill(refs[:sources], pool, sem):
        copy.wait()

    def one(row, carry):
        for k in range(count):
            held[row, k] = member_sum(members, pool, row, k)
        return carry

    lax.fori_loop(0, held.shape[0], one, 0)
    copy = pltpu.make_async_copy(held, out.at[:, pl.ds(first, count)], sem_out)
    copy.start()
    copy.wait()


def gather_rows(members, recv, so_far, shape, first, count):
    rows, _, width, _ = shape
    inputs = list(recv) + ([] if so_far is None else [so_far])
    slots = sum(part.shape[0] for part in recv)
    return pl.pallas_call(
        functools.partial(gather_kernel, first, count, len(recv)),
        out_shape=jax.ShapeDtypeStruct(shape, BF16),
        grid_spec=pltpu.PrefetchScalarGridSpec(
            num_scalar_prefetch=1,
            in_specs=[pl.BlockSpec(memory_space=ANY)] * len(inputs),
            out_specs=pl.BlockSpec(memory_space=ANY),
            scratch_shapes=[
                VMEM((slots, count, width, width), BF16),
                VMEM((rows, count, width, width), BF16),
                pltpu.SemaphoreType.DMA((len(recv),)),
                pltpu.SemaphoreType.DMA,
            ],
        ),
        input_output_aliases={} if so_far is None else {1 + len(recv): 0},
        compiler_params=LIMIT,
        cost_estimate=pl.CostEstimate(
            flops=2 * slots * count * width * width,
            bytes_accessed=3 * slots * count * width * width,
            transcendentals=0,
        ),
        name=f"gather_{first}",
    )(members, *inputs)


def block_row_product(coarse, pool, cols, row, count):
    total = None
    for k in range(0, count, 2):
        if k + 1 < count:
            lhs = jnp.concatenate([coarse[row, k], coarse[row, k + 1]], axis=1)
            rhs = jnp.concatenate([pool[cols[row, k]], pool[cols[row, k + 1]]], axis=0)
        else:
            lhs, rhs = coarse[row, k], pool[cols[row, k]]
        term = dot(lhs, rhs)
        total = term if total is None else total + term
    return total


def first_kernel(first, count, blocks, sources, members, cols, *refs):
    recv, refs = refs[:sources], refs[sources:]
    so_far, own, across, along, out, product, sent_a, sent_b, peak = refs[:9]
    slots, held, pool, sem, sem_in, sem_out = refs[9:]
    rows, width = product.shape[:2]
    half = sent_a.shape[0]
    copies = fill(recv, slots, sem)
    load = pltpu.make_async_copy(so_far.at[:, pl.ds(0, first)], held.at[:, pl.ds(0, first)], sem_in)
    load.start()
    for copy in copies:
        copy.wait()

    def last(row, carry):
        for k in range(count):
            held[row, first + k] = member_sum(members, slots, row, k)
        return carry

    lax.fori_loop(0, rows, last, 0)
    store = pltpu.make_async_copy(
        held.at[:, pl.ds(first, count)], out.at[:, pl.ds(first, count)], sem_out
    )
    store.start()
    load.wait()

    def sums(row, carry):
        total = jnp.abs(held[row, 0].astype(F32))
        for k in range(1, blocks):
            total = total + jnp.abs(held[row, k].astype(F32))
        return jnp.maximum(carry, jnp.sum(total, axis=1, keepdims=True))

    most = lax.fori_loop(0, rows, sums, jnp.zeros((width, 1), F32))
    most = jnp.max(most, axis=0, keepdims=True)
    peak[...] = jnp.broadcast_to(most[None], peak.shape)
    scale = 1.0 / jnp.clip(most, 2.0**-100, 2.0**120)
    for part, source in enumerate((own, across, along)):

        def scaled(row, carry):
            pool[part * rows + row] = (source[row].astype(F32) * scale).astype(BF16)
            return carry

        lax.fori_loop(0, rows, scaled, 0)
    for start, sent in ((0, sent_a), (half, sent_b)):

        def multiply(row, carry):
            total = block_row_product(held, pool, cols, start + row, blocks)
            product[start + row] = total
            sent[row] = total.astype(BF16)
            return carry

        lax.fori_loop(0, sent.shape[0], multiply, 0)
    store.wait()


def first_product(members, cols, recv, so_far, own, across, along, first, count, devices):
    rows, blocks, width, _ = so_far.shape
    half = (rows + 1) // 2
    vmem = pl.BlockSpec(memory_space=VMEM)
    hbm = pl.BlockSpec(memory_space=ANY)
    slots = sum(part.shape[0] for part in recv)
    return pl.pallas_call(
        functools.partial(first_kernel, first, count, blocks, len(recv)),
        out_shape=(
            jax.ShapeDtypeStruct(so_far.shape, BF16),
            jax.ShapeDtypeStruct(own.shape, F32),
            jax.ShapeDtypeStruct((half,) + own.shape[1:], BF16),
            jax.ShapeDtypeStruct((rows - half,) + own.shape[1:], BF16),
            jax.ShapeDtypeStruct((devices, 8, 128), F32),
        ),
        grid_spec=pltpu.PrefetchScalarGridSpec(
            num_scalar_prefetch=2,
            in_specs=[hbm] * (len(recv) + 1) + [vmem] * 3,
            out_specs=(hbm, vmem, vmem, vmem, vmem),
            scratch_shapes=[
                VMEM((slots, count, width, width), BF16),
                VMEM(so_far.shape, BF16),
                VMEM((3 * rows,) + own.shape[1:], BF16),
                pltpu.SemaphoreType.DMA((len(recv),)),
                pltpu.SemaphoreType.DMA,
                pltpu.SemaphoreType.DMA,
            ],
        ),
        input_output_aliases={2 + len(recv): 0},
        compiler_params=LIMIT,
        cost_estimate=pl.CostEstimate(
            flops=2 * so_far.size * own.shape[2],
            bytes_accessed=6 * so_far.size,
            transcendentals=0,
        ),
        name="first_product",
    )(members, cols, *recv, so_far, own, across, along)


def second_kernel(
    blocks, cols, near, coarse, own, across, along, product,
    across_a, across_b, along_a, along_b, peaks, out, pool,
):
    rows = out.shape[0]
    half = across_a.shape[0]
    largest = jnp.max(jnp.max(peaks[...], axis=0)[0:1], axis=1, keepdims=True)
    lower_end = largest / 30.0
    centre = (largest + lower_end) / 2.0
    half_width = (largest - lower_end) / 2.0
    sigma = centre / half_width
    weight_0 = 1.0 / sigma
    weight_1 = 1.0 / (2.0 * sigma - weight_0)
    weight_2 = 1.0 / (2.0 * sigma - weight_1)
    start = 1.0 / centre
    gain_1 = 2.0 * weight_1 / half_width
    gain_2 = 2.0 * weight_2 / half_width
    change = weight_1 * weight_0 * start + gain_1

    def back(slot):
        peak = peaks[near[slot]][0:1, 0:1]
        return gain_1 * (jnp.clip(peak, 2.0**-100, 2.0**120) / centre)

    pieces = (
        (0, 0, own, product),
        (1, 0, across, across_a),
        (1, half, across, across_b),
        (2, 0, along, along_a),
        (2, half, along, along_b),
    )
    for part, start_row, source, seen in pieces:
        factor = back(part)

        def iterate(row, carry):
            at = start_row + row
            value = (start + change) * source[at].astype(F32) - factor * seen[row].astype(F32)
            pool[part * rows + at] = value.astype(BF16)
            return carry

        lax.fori_loop(0, seen.shape[0], iterate, 0)
    mine = back(0)

    def multiply(row, carry):
        right = own[row].astype(F32)
        update = change * right - mine * product[row]
        residual = right - block_row_product(coarse, pool, cols, row, blocks)
        value = start * right + update + (weight_2 * weight_1 * update + gain_2 * residual)
        out[row] = value.astype(BF16)
        return carry

    lax.fori_loop(0, rows, multiply, 0)


def second_product(cols, near, coarse, own, across, along, product, seen, peaks):
    rows, blocks, _, _ = coarse.shape
    vmem = pl.BlockSpec(memory_space=VMEM)
    return pl.pallas_call(
        functools.partial(second_kernel, blocks),
        out_shape=jax.ShapeDtypeStruct(own.shape, BF16),
        grid_spec=pltpu.PrefetchScalarGridSpec(
            num_scalar_prefetch=2,
            in_specs=[vmem] * 10,
            out_specs=vmem,
            scratch_shapes=[VMEM((3 * rows,) + own.shape[1:], BF16)],
        ),
        compiler_params=LIMIT,
        cost_estimate=pl.CostEstimate(
            flops=2 * coarse.size * own.shape[2],
            bytes_accessed=6 * coarse.size,
            transcendentals=0,
        ),
        name="second_product",
    )(cols, near, coarse, own, across, along, product, *seen, peaks)


def exchange(block, axis):
    return lax.all_to_all(block, axis, split_axis=0, concat_axis=0, tiled=True)


def shifted(block, offset):
    count = lax.axis_size("gy")
    return lax.ppermute(block, "gy", [(i, (i + offset) % count) for i in range(count)])


def to_partner(block):
    count = lax.axis_size("gy")
    return lax.ppermute(block, "gy", [(i, i ^ 1) for i in range(count) if i ^ 1 < count])


def pass_on(block):
    count = lax.axis_size("gy")
    steps = [(i, i + 2 if i % 2 == 0 else i - 2) for i in range(count)]
    return lax.ppermute(block, "gy", [(i, to) for i, to in steps if 0 <= to < count])


def to_other(block):
    count = lax.axis_size("gy")
    steps = [(i, i - 1 if i % 2 == 0 else i + 1) for i in range(count)]
    return lax.ppermute(block, "gy", [(i, to) for i, to in steps if 0 <= to < count])


def routes(fine_agg, balance, coarse_rows):
    group = lax.axis_size("gy")
    me = lax.axis_index("gy")
    rows = fine_agg.shape[0]
    facts = jnp.concatenate([fine_agg, balance.reshape(-1)])
    facts = exchange(jnp.broadcast_to(facts[None], (group,) + facts.shape), "gy")
    named, table = facts[:, :rows], facts[:, rows:].reshape(-1)
    keys = jnp.arange(table.shape[0], dtype=jnp.int32)
    target = jnp.sum(
        jnp.where(named[:, :, None] == keys[None, None, :], table[None, None, :], 0), axis=2
    )
    device = target // coarse_rows
    before = jnp.arange(rows)[:, None] > jnp.arange(rows)[None, :]
    rank = jnp.sum(
        ((device[:, :, None] == device[:, None, :]) & before[None]).astype(jnp.int32), axis=2
    )
    mine = (jnp.arange(group) == me)[:, None]
    place = jnp.sum(jnp.where(mine, (device - me) % group * OCAP + rank, 0), axis=0)
    slots = jnp.arange(group * OCAP, dtype=jnp.int32)
    order = jnp.sum(
        jnp.where(place[None, :] == slots[:, None], jnp.arange(rows, dtype=jnp.int32)[None, :], 0),
        axis=1,
    )
    goal = me * coarse_rows + jnp.arange(coarse_rows, dtype=jnp.int32)
    hit = target[None] == goal[:, None, None]
    slot = (me - jnp.arange(group, dtype=jnp.int32))[:, None] % group * OCAP + rank
    source = jnp.sum(jnp.where(hit, slot[None] + 1, 0), axis=2)
    found = (source > 0).astype(jnp.int32)
    earlier = jnp.arange(group)[:, None] < jnp.arange(group)[None, :]
    ordinal = jnp.sum(found[:, :, None] * earlier[None].astype(jnp.int32), axis=1)
    members = jnp.stack(
        [
            jnp.sum(jnp.where((ordinal == m) & (found > 0), source - 1, 0), axis=1)
            for m in range(MEMBERS)
        ],
        axis=1,
    )
    return order.astype(jnp.int32), members.astype(jnp.int32)


def per_device(a_blocks, prolong, neighbour, ghost_send, fine_agg, balance, coarse_cols, loads):
    block_rows, blocks = a_blocks.shape[:2]
    group = lax.axis_size("gy")
    row_gy = lax.axis_index("gy")
    row_gx = lax.axis_index("gx")
    devices = group * lax.axis_size("gx")
    coarse_rows = loads.shape[0]
    width = prolong.shape[2]
    cap = ghost_send.shape[3]
    offsets = range(1, group)

    across = to_partner(loads)
    picked = pick_ghosts(row_gy.astype(jnp.int32)[None], ghost_send[0, 0], prolong)
    arrived = [shifted(block, offset) for offset, block in zip(offsets, picked)]
    along = pass_on(across)
    fine_agg, _ = lax.optimization_barrier((fine_agg, picked[0]))
    order, members = routes(fine_agg, balance, coarse_rows)
    remote = neighbour - block_rows
    offset = (row_gy - remote // cap) % group
    neighbour = jnp.where(
        remote < 0, neighbour, block_rows + (offset - 1) * cap + remote % cap
    )
    columns = jnp.concatenate(
        [jnp.arange(block_rows, dtype=jnp.int32)[:, None], neighbour], axis=1
    )
    parts = chunks_of(blocks)
    received, after = [], []
    for first, count in parts:
        sources = [prolong] if (first, count) == (0, 1) else [prolong] + arrived
        sent = galerkin(a_blocks, sources, after, order, columns, first, count)
        after = sent[:1]
        received.append(
            [sent[0]] + [shifted(block, offset) for offset, block in zip(offsets, sent[1:])]
        )
    so_far = None
    for (first, count), recv in zip(parts[:-1], received[:-1]):
        so_far = gather_rows(
            members, recv, so_far, (coarse_rows, blocks, width, width), first, count
        )
    beside = coarse_cols // coarse_rows - (row_gx * group + row_gy)
    toward = 1 - 2 * (row_gy % 2)
    part = jnp.where(beside == 0, 0, jnp.where(beside == toward, 1, 2))
    local_cols = part * coarse_rows + coarse_cols % coarse_rows
    coarse, product, sent_a, sent_b, peak = first_product(
        members, local_cols, received[-1], so_far, loads, across, along, *parts[-1], devices
    )
    across_a = to_partner(sent_a)
    across_b = to_partner(sent_b)
    along_b = to_other(sent_b)
    along_a = pass_on(across_a)
    peaks = exchange(peak, ("gx", "gy"))
    here = row_gx * group + row_gy
    near = jnp.clip(jnp.stack([here, here + toward, here - toward]), 0, devices - 1)
    smoothed = second_product(
        local_cols,
        near.astype(jnp.int32),
        coarse,
        loads,
        across,
        along,
        product,
        (across_a, across_b, along_a, along_b),
        peaks,
    )
    return coarse, smoothed


def solution(mesh):
    return jax.shard_map(
        per_device,
        mesh=mesh,
        in_specs=(
            P(("gx", "gy"), None, None, None),
            P(("gx", "gy"), None, None),
            P(("gx", "gy"), None),
            P("gx", "gy", None, None),
            P(("gx", "gy")),
            P("gx", "gy", None),
            P(("gx", "gy"), None),
            P(("gx", "gy"), None, None),
        ),
        out_specs=(P(("gx", "gy"), None, None, None), P(("gx", "gy"), None, None)),
        check_vma=False,
    )
```

```python
import functools

import jax
import jax.numpy as jnp
from jax import lax
from jax.experimental import pallas as pl
from jax.experimental.pallas import tpu as pltpu
from jax.sharding import PartitionSpec as P


OCAP = 3
MEMBERS = 3
CHUNKS = (1, 3, 2, 1)

F32 = jnp.float32
BF16 = jnp.bfloat16
VMEM = pltpu.VMEM
ANY = pl.ANY


LIMIT = pltpu.CompilerParams(vmem_limit_bytes=24 << 20)
WIDE = pltpu.CompilerParams(vmem_limit_bytes=46 << 20)


def chunks_of(count):
    parts, at = [], 0
    for size in CHUNKS[:-1]:
        size = min(size, count - at - 1)
        if size > 0:
            parts.append((at, size))
            at += size
    return parts + [(at, count - at)]


def dot(a, b):
    return lax.dot_general(a, b, (((1,), (0,)), ((), ())), preferred_element_type=F32)


def pick_kernel(group, cap, me, wanted, prolong, *refs):
    outs, sem = refs[:-1], refs[-1]
    copies = []
    for offset in range(1, group):
        peer = lax.rem(me[0] + offset, group)
        for c in range(cap):
            copies.append(
                pltpu.make_async_copy(
                    prolong.at[wanted[peer, c]], outs[offset - 1].at[c], sem.at[len(copies)]
                )
            )
            copies[-1].start()
    for copy in copies:
        copy.wait()


def pick_ghosts(me, wanted, prolong):
    group, cap = wanted.shape
    shape = jax.ShapeDtypeStruct((cap,) + prolong.shape[1:], BF16)
    vmem = pl.BlockSpec(memory_space=VMEM)
    return pl.pallas_call(
        functools.partial(pick_kernel, group, cap),
        out_shape=[shape] * (group - 1),
        grid_spec=pltpu.PrefetchScalarGridSpec(
            num_scalar_prefetch=2,
            in_specs=[pl.BlockSpec(memory_space=pltpu.HBM)],
            out_specs=[vmem] * (group - 1),
            scratch_shapes=[pltpu.SemaphoreType.DMA(((group - 1) * cap,))],
        ),
        compiler_params=LIMIT,
        cost_estimate=pl.CostEstimate(
            flops=0, bytes_accessed=4 * prolong.size, transcendentals=0
        ),
        name="pick_ghosts",
    )(me, wanted, prolong)


def fill(sources, pool, sem, at=0):
    copies = []
    for source in sources:
        size = source.shape[0]
        copies.append(pltpu.make_async_copy(source, pool.at[pl.ds(at, size)], sem.at[len(copies)]))
        at += size
    for copy in copies:
        copy.start()
    return copies


def galerkin_kernel(first, count, group, given, order, cols, a_blocks, *refs):
    sources, refs = refs[:given], refs[given:]
    outs, refs = refs[:group], refs[group:]
    if first == 0:
        turned_out, turned, blocks, pool, done, sem_a, sem, sem_out, sem_turned = refs
    else:
        turned, blocks, pool, done, sem_a, sem, sem_out = refs
        sources, turned_in = sources[1:], sources[0]

    def fetch(slot):
        return pltpu.make_async_copy(
            a_blocks.at[order[slot], pl.ds(first, count)], blocks.at[slot], sem_a.at[slot]
        )

    fills = fill(sources, pool, sem)
    if first > 0:
        fills.append(pltpu.make_async_copy(turned_in, turned, sem.at[len(fills)]))
        fills[-1].start()

    def begin(slot, carry):
        fetch(slot).start()
        return carry

    lax.fori_loop(0, group * OCAP, begin, 0)
    for copy in fills:
        copy.wait()
    width = done.shape[-1]

    together = max(1, min(group, 4 if count < 3 else 2))

    def some_offsets(turn, carry):
        slots = [turn * together * OCAP + s for s in range(together * OCAP)]
        for slot in slots:
            fetch(slot).wait()
        applied = [
            [
                dot(blocks[slot, k], pool[cols[order[slot], first + k]]).astype(BF16)
                for k in range(count)
            ]
            for slot in slots
        ]
        for s, slot in enumerate(slots):
            row = order[slot]
            at, place = turn * together + s // OCAP, s % OCAP
            if first == 0:
                left = pool[row].T
                turned[row] = left
            else:
                left = turned[row]
            for k in range(0, count, 2):
                if k + 1 < count:
                    both = jnp.concatenate(applied[s][k : k + 2], axis=1)
                    both = dot(left, both).astype(BF16)
                    done[at, place, k] = both[:, :width]
                    done[at, place, k + 1] = both[:, width:]
                else:
                    done[at, place, k] = dot(left, applied[s][k]).astype(BF16)
        for to in range(group):

            @pl.when(turn == to // together)
            def send():
                pltpu.make_async_copy(done.at[to], outs[to], sem_out.at[to]).start()

        return carry

    lax.fori_loop(0, group // together, some_offsets, 0)
    if first == 0:
        store = pltpu.make_async_copy(turned, turned_out, sem_turned)
        store.start()
    for to in range(group):
        pltpu.make_async_copy(done.at[to], outs[to], sem_out.at[to]).wait()
    if first == 0:
        store.wait()


def galerkin(a_blocks, sources, turned, order, cols, first, count):
    rows, _, size, _ = a_blocks.shape
    width = sources[0].shape[2]
    slots = order.shape[0]
    group = slots // OCAP
    out = jax.ShapeDtypeStruct((OCAP, count, width, width), BF16)
    turned_shape = jax.ShapeDtypeStruct((rows, width, size), BF16)
    outs = [out] * group + ([turned_shape] if turned is None else [])
    inputs = list(sources) if turned is None else [turned] + list(sources)
    held = sum(source.shape[0] for source in sources)
    hbm = pl.BlockSpec(memory_space=pltpu.HBM)
    return pl.pallas_call(
        functools.partial(galerkin_kernel, first, count, group, len(inputs)),
        out_shape=outs,
        grid_spec=pltpu.PrefetchScalarGridSpec(
            num_scalar_prefetch=2,
            in_specs=[hbm] + [pl.BlockSpec(memory_space=ANY)] * len(inputs),
            out_specs=[pl.BlockSpec(memory_space=ANY)] * len(outs),
            scratch_shapes=[
                VMEM(turned_shape.shape, BF16),
                VMEM((slots, count, size, size), BF16),
                VMEM((held, size, width), BF16),
                VMEM((group,) + out.shape, BF16),
                pltpu.SemaphoreType.DMA((slots,)),
                pltpu.SemaphoreType.DMA((len(inputs),)),
                pltpu.SemaphoreType.DMA((group,)),
            ]
            + ([pltpu.SemaphoreType.DMA] if turned is None else []),
        ),
        compiler_params=WIDE,
        cost_estimate=pl.CostEstimate(
            flops=2 * slots * count * (size * size * width + size * width * width),
            bytes_accessed=2 * slots * count * (size * size + width * width),
            transcendentals=0,
        ),
    )(order, cols, a_blocks, *inputs)


def member_sum(members, pool, row, k):
    total = pool[members[row, 0], k].astype(F32)
    for m in range(1, MEMBERS):
        total = total + pool[members[row, m], k].astype(F32)
    return total.astype(BF16)


def gather_kernel(first, count, sources, members, *refs):
    out, pool, held, sem, sem_out = refs[-5:]
    for copy in fill(refs[:sources], pool, sem):
        copy.wait()

    def one(row, carry):
        for k in range(count):
            held[row, k] = member_sum(members, pool, row, k)
        return carry

    lax.fori_loop(0, held.shape[0], one, 0, unroll=True)
    copy = pltpu.make_async_copy(held, out.at[:, pl.ds(first, count)], sem_out)
    copy.start()
    copy.wait()


def gather_rows(members, recv, so_far, shape, first, count):
    rows, _, width, _ = shape
    inputs = list(recv) + ([] if so_far is None else [so_far])
    slots = sum(part.shape[0] for part in recv)
    return pl.pallas_call(
        functools.partial(gather_kernel, first, count, len(recv)),
        out_shape=jax.ShapeDtypeStruct(shape, BF16),
        grid_spec=pltpu.PrefetchScalarGridSpec(
            num_scalar_prefetch=1,
            in_specs=[pl.BlockSpec(memory_space=ANY)] * len(inputs),
            out_specs=pl.BlockSpec(memory_space=ANY),
            scratch_shapes=[
                VMEM((slots, count, width, width), BF16),
                VMEM((rows, count, width, width), BF16),
                pltpu.SemaphoreType.DMA((len(recv),)),
                pltpu.SemaphoreType.DMA,
            ],
        ),
        input_output_aliases={} if so_far is None else {1 + len(recv): 0},
        compiler_params=LIMIT,
        cost_estimate=pl.CostEstimate(
            flops=2 * slots * count * width * width,
            bytes_accessed=3 * slots * count * width * width,
            transcendentals=0,
        ),
    )(members, *inputs)


def block_row_product(coarse, pool, cols, row, count):
    total = None
    for k in range(0, count, 2):
        if k + 1 < count:
            lhs = jnp.concatenate([coarse[row, k], coarse[row, k + 1]], axis=1)
            rhs = jnp.concatenate([pool[cols[row, k]], pool[cols[row, k + 1]]], axis=0)
        else:
            lhs, rhs = coarse[row, k], pool[cols[row, k]]
        term = dot(lhs, rhs)
        total = term if total is None else total + term
    return total


def first_kernel(first, count, blocks, sources, members, cols, *refs):
    recv, refs = refs[:sources], refs[sources:]
    so_far, own, across, along, out, product, sent_a, sent_b, peak = refs[:9]
    slots, held, pool, sem, sem_in, sem_out = refs[9:]
    rows, width = product.shape[:2]
    half = sent_a.shape[0]
    copies = fill(recv, slots, sem)
    load = pltpu.make_async_copy(so_far.at[:, pl.ds(0, first)], held.at[:, pl.ds(0, first)], sem_in)
    load.start()
    for copy in copies:
        copy.wait()

    def last(row, carry):
        for k in range(count):
            held[row, first + k] = member_sum(members, slots, row, k)
        return carry

    lax.fori_loop(0, rows, last, 0, unroll=True)
    store = pltpu.make_async_copy(
        held.at[:, pl.ds(first, count)], out.at[:, pl.ds(first, count)], sem_out
    )
    store.start()
    load.wait()

    def sums(row, carry):
        total = jnp.abs(held[row, 0].astype(F32))
        for k in range(1, blocks):
            total = total + jnp.abs(held[row, k].astype(F32))
        return jnp.maximum(carry, jnp.sum(total, axis=1, keepdims=True))

    most = lax.fori_loop(0, rows, sums, jnp.zeros((width, 1), F32), unroll=True)
    most = jnp.max(most, axis=0, keepdims=True)
    peak[...] = jnp.broadcast_to(most[None], peak.shape)
    scale = 1.0 / jnp.clip(most, 2.0**-100, 2.0**120)
    for part, source in enumerate((own, across, along)):

        def scaled(row, carry):
            pool[part * rows + row] = (source[row].astype(F32) * scale).astype(BF16)
            return carry

        lax.fori_loop(0, rows, scaled, 0, unroll=True)
    for start, sent in ((0, sent_a), (half, sent_b)):

        def multiply(row, carry):
            total = block_row_product(held, pool, cols, start + row, blocks)
            product[start + row] = total
            sent[row] = total.astype(BF16)
            return carry

        lax.fori_loop(0, sent.shape[0], multiply, 0, unroll=True)
    store.wait()


def first_product(members, cols, recv, so_far, own, across, along, first, count, devices):
    rows, blocks, width, _ = so_far.shape
    half = (rows + 1) // 2
    vmem = pl.BlockSpec(memory_space=VMEM)
    hbm = pl.BlockSpec(memory_space=ANY)
    slots = sum(part.shape[0] for part in recv)
    return pl.pallas_call(
        functools.partial(first_kernel, first, count, blocks, len(recv)),
        out_shape=(
            jax.ShapeDtypeStruct(so_far.shape, BF16),
            jax.ShapeDtypeStruct(own.shape, F32),
            jax.ShapeDtypeStruct((half,) + own.shape[1:], BF16),
            jax.ShapeDtypeStruct((rows - half,) + own.shape[1:], BF16),
            jax.ShapeDtypeStruct((devices, 8, 128), F32),
        ),
        grid_spec=pltpu.PrefetchScalarGridSpec(
            num_scalar_prefetch=2,
            in_specs=[hbm] * (len(recv) + 1) + [vmem] * 3,
            out_specs=(hbm, vmem, vmem, vmem, vmem),
            scratch_shapes=[
                VMEM((slots, count, width, width), BF16),
                VMEM(so_far.shape, BF16),
                VMEM((3 * rows,) + own.shape[1:], BF16),
                pltpu.SemaphoreType.DMA((len(recv),)),
                pltpu.SemaphoreType.DMA,
                pltpu.SemaphoreType.DMA,
            ],
        ),
        input_output_aliases={2 + len(recv): 0},
        compiler_params=LIMIT,
        cost_estimate=pl.CostEstimate(
            flops=2 * so_far.size * own.shape[2],
            bytes_accessed=6 * so_far.size,
            transcendentals=0,
        ),
        name="first_product",
    )(members, cols, *recv, so_far, own, across, along)


def second_kernel(
    blocks, cols, near, coarse_hbm, own, across, along, product,
    across_a, across_b, along_a, along_b, peaks, out, pool, coarse, sem,
):
    rows = out.shape[0]
    half = across_a.shape[0]
    load = pltpu.make_async_copy(coarse_hbm, coarse, sem)
    load.start()
    largest = jnp.max(jnp.max(peaks[...], axis=0)[0:1], axis=1, keepdims=True)
    lower_end = largest / 30.0
    centre = (largest + lower_end) / 2.0
    half_width = (largest - lower_end) / 2.0
    sigma = centre / half_width
    weight_0 = 1.0 / sigma
    weight_1 = 1.0 / (2.0 * sigma - weight_0)
    weight_2 = 1.0 / (2.0 * sigma - weight_1)
    start = 1.0 / centre
    gain_1 = 2.0 * weight_1 / half_width
    gain_2 = 2.0 * weight_2 / half_width
    change = weight_1 * weight_0 * start + gain_1

    def back(slot):
        peak = peaks[near[slot]][0:1, 0:1]
        return gain_1 * (jnp.clip(peak, 2.0**-100, 2.0**120) / centre)

    pieces = (
        (0, 0, own, product),
        (1, 0, across, across_a),
        (1, half, across, across_b),
        (2, 0, along, along_a),
        (2, half, along, along_b),
    )
    for part, start_row, source, seen in pieces:
        factor = back(part)

        def iterate(row, carry):
            at = start_row + row
            value = (start + change) * source[at].astype(F32) - factor * seen[row].astype(F32)
            pool[part * rows + at] = value.astype(BF16)
            return carry

        lax.fori_loop(0, seen.shape[0], iterate, 0, unroll=True)
    mine = back(0)
    load.wait()

    def multiply(row, carry):
        right = own[row].astype(F32)
        update = change * right - mine * product[row]
        residual = right - block_row_product(coarse, pool, cols, row, blocks)
        value = start * right + update + (weight_2 * weight_1 * update + gain_2 * residual)
        out[row] = value.astype(BF16)
        return carry

    lax.fori_loop(0, rows, multiply, 0, unroll=True)


def second_product(cols, near, coarse, own, across, along, product, seen, peaks):
    rows, blocks, _, _ = coarse.shape
    vmem = pl.BlockSpec(memory_space=VMEM)
    return pl.pallas_call(
        functools.partial(second_kernel, blocks),
        out_shape=jax.ShapeDtypeStruct(own.shape, BF16),
        grid_spec=pltpu.PrefetchScalarGridSpec(
            num_scalar_prefetch=2,
            in_specs=[pl.BlockSpec(memory_space=pltpu.HBM)] + [vmem] * 9,
            out_specs=vmem,
            scratch_shapes=[
                VMEM((3 * rows,) + own.shape[1:], BF16),
                VMEM(coarse.shape, BF16),
                pltpu.SemaphoreType.DMA,
            ],
        ),
        compiler_params=LIMIT,
        cost_estimate=pl.CostEstimate(
            flops=2 * coarse.size * own.shape[2],
            bytes_accessed=6 * coarse.size,
            transcendentals=0,
        ),
        name="second_product",
    )(cols, near, coarse, own, across, along, product, *seen, peaks)


def exchange(block, axis):
    return lax.all_to_all(block, axis, split_axis=0, concat_axis=0, tiled=True)


def shifted(block, offset):
    count = lax.axis_size("gy")
    return lax.ppermute(block, "gy", [(i, (i + offset) % count) for i in range(count)])


def to_partner(block):
    count = lax.axis_size("gy")
    return lax.ppermute(block, "gy", [(i, i ^ 1) for i in range(count) if i ^ 1 < count])


def pass_on(block):
    count = lax.axis_size("gy")
    steps = [(i, i + 2 if i % 2 == 0 else i - 2) for i in range(count)]
    return lax.ppermute(block, "gy", [(i, to) for i, to in steps if 0 <= to < count])


def past_partner(block):
    count = lax.axis_size("gy")
    steps = [(i, i - 2 if i % 2 == 0 else i + 2) for i in range(count)]
    return lax.ppermute(block, "gy", [(i, to) for i, to in steps if 0 <= to < count])


def to_other(block):
    count = lax.axis_size("gy")
    steps = [(i, i - 1 if i % 2 == 0 else i + 1) for i in range(count)]
    return lax.ppermute(block, "gy", [(i, to) for i, to in steps if 0 <= to < count])


def routes(fine_agg, balance, coarse_rows):
    group = lax.axis_size("gy")
    me = lax.axis_index("gy")
    rows = fine_agg.shape[0]
    facts = jnp.concatenate([fine_agg, balance.reshape(-1)])
    facts = exchange(jnp.broadcast_to(facts[None, None], (group, 1) + facts.shape), "gy")[:, 0]
    named, table = facts[:, :rows], facts[:, rows:].reshape(-1)
    keys = jnp.arange(table.shape[0], dtype=jnp.int32)
    target = jnp.sum(
        jnp.where(named[:, :, None] == keys[None, None, :], table[None, None, :], 0), axis=2
    )
    device = target // coarse_rows
    before = jnp.arange(rows)[:, None] > jnp.arange(rows)[None, :]
    rank = jnp.sum(
        ((device[:, :, None] == device[:, None, :]) & before[None]).astype(jnp.int32), axis=2
    )
    mine = (jnp.arange(group) == me)[:, None]
    place = jnp.sum(jnp.where(mine, (device - me) % group * OCAP + rank, 0), axis=0)
    slots = jnp.arange(group * OCAP, dtype=jnp.int32)
    order = jnp.sum(
        jnp.where(place[None, :] == slots[:, None], jnp.arange(rows, dtype=jnp.int32)[None, :], 0),
        axis=1,
    )
    goal = me * coarse_rows + jnp.arange(coarse_rows, dtype=jnp.int32)
    hit = target[None] == goal[:, None, None]
    slot = (me - jnp.arange(group, dtype=jnp.int32))[:, None] % group * OCAP + rank
    source = jnp.sum(jnp.where(hit, slot[None] + 1, 0), axis=2)
    found = (source > 0).astype(jnp.int32)
    earlier = jnp.arange(group)[:, None] < jnp.arange(group)[None, :]
    ordinal = jnp.sum(found[:, :, None] * earlier[None].astype(jnp.int32), axis=1)
    members = jnp.stack(
        [
            jnp.sum(jnp.where((ordinal == m) & (found > 0), source - 1, 0), axis=1)
            for m in range(MEMBERS)
        ],
        axis=1,
    )
    return order.astype(jnp.int32), members.astype(jnp.int32)


def step(a_blocks, prolong, neighbour, ghost_send, fine_agg, balance, coarse_cols, loads):
    block_rows, blocks = a_blocks.shape[:2]
    group = lax.axis_size("gy")
    row_gy = lax.axis_index("gy")
    row_gx = lax.axis_index("gx")
    devices = group * lax.axis_size("gx")
    coarse_rows = loads.shape[0]
    width = prolong.shape[2]
    cap = ghost_send.shape[3]
    offsets = range(1, group)

    beyond = past_partner(loads)
    picked = pick_ghosts(row_gy.astype(jnp.int32)[None], ghost_send[0, 0], prolong)
    arrived = [shifted(block, offset) for offset, block in zip(offsets, picked)]
    across = to_partner(loads)
    along = to_partner(beyond)
    order, members = routes(fine_agg, balance, coarse_rows)
    remote = neighbour - block_rows
    offset = (row_gy - remote // cap) % group
    neighbour = jnp.where(
        remote < 0, neighbour, block_rows + (offset - 1) * cap + remote % cap
    )
    columns = jnp.concatenate(
        [jnp.arange(block_rows, dtype=jnp.int32)[:, None], neighbour], axis=1
    )
    parts = chunks_of(blocks)
    received, turned = [], None
    for first, count in parts:
        sources = [prolong] + (arrived if first > 0 else [])
        sent = list(galerkin(a_blocks, sources, turned, order, columns, first, count))
        turned = sent.pop() if first == 0 else turned
        received.append(
            sent[:1] + [shifted(block, offset) for offset, block in zip(offsets, sent[1:])]
        )
    so_far = None
    for (first, count), recv in zip(parts[:-1], received[:-1]):
        shape = (coarse_rows, blocks, width, width)
        so_far = gather_rows(members, recv, so_far, shape, first, count)
    beside = coarse_cols // coarse_rows - (row_gx * group + row_gy)
    toward = 1 - 2 * (row_gy % 2)
    part = jnp.where(beside == 0, 0, jnp.where(beside == toward, 1, 2))
    local_cols = part * coarse_rows + coarse_cols % coarse_rows
    coarse, product, sent_a, sent_b, peak = first_product(
        members, local_cols, received[-1], so_far, loads, across, along, *parts[-1], devices
    )
    across_a = to_partner(sent_a)
    across_b = to_partner(sent_b)
    along_b = to_other(sent_b)
    along_a = pass_on(across_a)
    peaks = exchange(peak, ("gx", "gy"))
    here = row_gx * group + row_gy
    near = jnp.clip(jnp.stack([here, here + toward, here - toward]), 0, devices - 1)
    smoothed = second_product(
        local_cols,
        near.astype(jnp.int32),
        coarse,
        loads,
        across,
        along,
        product,
        (across_a, across_b, along_a, along_b),
        peaks,
    )
    return coarse, smoothed


def solution(mesh):
    return jax.shard_map(
        step,
        mesh=mesh,
        in_specs=(
            P(("gx", "gy"), None, None, None),
            P(("gx", "gy"), None, None),
            P(("gx", "gy"), None),
            P("gx", "gy", None, None),
            P(("gx", "gy")),
            P("gx", "gy", None),
            P(("gx", "gy"), None),
            P(("gx", "gy"), None, None),
        ),
        out_specs=(P(("gx", "gy"), None, None, None), P(("gx", "gy"), None, None)),
        check_vma=False,
    )
```

```python
import functools

import jax
import jax.numpy as jnp
from jax import lax
from jax.experimental import pallas as pl
from jax.experimental.pallas import tpu as pltpu
from jax.sharding import PartitionSpec as P


OCAP = 3
MEMBERS = 3
CHUNKS = (1, 2, 3, 1)

F32 = jnp.float32
BF16 = jnp.bfloat16
VMEM = pltpu.VMEM
ANY = pl.ANY


LIMIT = pltpu.CompilerParams(vmem_limit_bytes=12 << 20)
WIDE = pltpu.CompilerParams(vmem_limit_bytes=46 << 20)


def chunks_of(count):
    parts, at = [], 0
    for size in CHUNKS[:-1]:
        size = min(size, count - at - 1)
        if size > 0:
            parts.append((at, size))
            at += size
    return parts + [(at, count - at)]


def in_hbm(block):
    return pltpu.with_memory_space_constraint(block, pltpu.HBM)


def dot(a, b):
    return lax.dot_general(a, b, (((1,), (0,)), ((), ())), preferred_element_type=F32)


def pick_kernel(group, cap, me, wanted, prolong, *refs):
    outs, sem = refs[:-1], refs[-1]
    copies = []
    for offset in range(1, group):
        peer = lax.rem(me[0] + offset, group)
        for c in range(cap):
            copies.append(
                pltpu.make_async_copy(
                    prolong.at[wanted[peer, c]], outs[offset - 1].at[c], sem.at[len(copies)]
                )
            )
            copies[-1].start()
    for copy in copies:
        copy.wait()


def pick_ghosts(me, wanted, prolong):
    group, cap = wanted.shape
    shape = jax.ShapeDtypeStruct((cap,) + prolong.shape[1:], BF16)
    vmem = pl.BlockSpec(memory_space=VMEM)
    return pl.pallas_call(
        functools.partial(pick_kernel, group, cap),
        out_shape=[shape] * (group - 1),
        grid_spec=pltpu.PrefetchScalarGridSpec(
            num_scalar_prefetch=2,
            in_specs=[pl.BlockSpec(memory_space=pltpu.HBM)],
            out_specs=[vmem] * (group - 1),
            scratch_shapes=[pltpu.SemaphoreType.DMA(((group - 1) * cap,))],
        ),
        cost_estimate=pl.CostEstimate(
            flops=0, bytes_accessed=4 * prolong.size, transcendentals=0
        ),
        name="pick_ghosts",
    )(me, wanted, prolong)


def fill(sources, pool, sem, at=0):
    copies = []
    for source in sources:
        size = source.shape[0]
        copies.append(pltpu.make_async_copy(source, pool.at[pl.ds(at, size)], sem.at[len(copies)]))
        at += size
    for copy in copies:
        copy.start()
    return copies


def galerkin_kernel(first, count, group, given, order, cols, a_blocks, *refs):
    sources, refs = refs[:given], refs[given:]
    outs, refs = refs[:group], refs[group:]
    if first == 0:
        turned_out, turned, blocks, pool, done, sem_a, sem, sem_out, sem_turned = refs
    else:
        turned, blocks, pool, done, sem_a, sem, sem_out = refs
        sources, turned_in = sources[1:], sources[0]

    def fetch(slot):
        return pltpu.make_async_copy(
            a_blocks.at[order[slot], pl.ds(first, count)], blocks.at[slot], sem_a.at[slot]
        )

    fills = fill(sources, pool, sem)
    if first > 0:
        fills.append(pltpu.make_async_copy(turned_in, turned, sem.at[len(fills)]))
        fills[-1].start()

    def begin(slot, carry):
        fetch(slot).start()
        return carry

    lax.fori_loop(0, group * OCAP, begin, 0)
    for copy in fills:
        copy.wait()
    width = done.shape[-1]

    together = max(1, min(group, 4 if count < 3 else 2))

    def some_offsets(turn, carry):
        slots = [turn * together * OCAP + s for s in range(together * OCAP)]
        for slot in slots:
            fetch(slot).wait()
        applied = [
            [
                dot(blocks[slot, k], pool[cols[order[slot], first + k]]).astype(BF16)
                for k in range(count)
            ]
            for slot in slots
        ]
        for s, slot in enumerate(slots):
            row = order[slot]
            at, place = turn * together + s // OCAP, s % OCAP
            if first == 0:
                left = pool[row].T
                turned[row] = left
            else:
                left = turned[row]
            for k in range(0, count, 2):
                if k + 1 < count:
                    both = jnp.concatenate(applied[s][k : k + 2], axis=1)
                    both = dot(left, both).astype(BF16)
                    done[at, place, k] = both[:, :width]
                    done[at, place, k + 1] = both[:, width:]
                else:
                    done[at, place, k] = dot(left, applied[s][k]).astype(BF16)
        for to in range(group):

            @pl.when(turn == to // together)
            def send():
                pltpu.make_async_copy(done.at[to], outs[to], sem_out.at[to]).start()

        return carry

    lax.fori_loop(0, group // together, some_offsets, 0)
    if first == 0:
        store = pltpu.make_async_copy(turned, turned_out, sem_turned)
        store.start()
    for to in range(group):
        pltpu.make_async_copy(done.at[to], outs[to], sem_out.at[to]).wait()
    if first == 0:
        store.wait()


def galerkin(a_blocks, sources, turned, order, cols, first, count):
    rows, _, size, _ = a_blocks.shape
    width = sources[0].shape[2]
    slots = order.shape[0]
    group = slots // OCAP
    out = pltpu.HBM((OCAP, count, width, width), BF16)
    turned_shape = jax.ShapeDtypeStruct((rows, width, size), BF16)
    outs = [out] * group + ([turned_shape] if turned is None else [])
    inputs = list(sources) if turned is None else [turned] + list(sources)
    held = sum(source.shape[0] for source in sources)
    hbm = pl.BlockSpec(memory_space=pltpu.HBM)
    return pl.pallas_call(
        functools.partial(galerkin_kernel, first, count, group, len(inputs)),
        out_shape=outs,
        grid_spec=pltpu.PrefetchScalarGridSpec(
            num_scalar_prefetch=2,
            in_specs=[hbm] + [pl.BlockSpec(memory_space=ANY)] * len(inputs),
            out_specs=[pl.BlockSpec(memory_space=ANY)] * len(outs),
            scratch_shapes=[
                VMEM(turned_shape.shape, BF16),
                VMEM((slots, count, size, size), BF16),
                VMEM((held, size, width), BF16),
                VMEM((group,) + out.shape, BF16),
                pltpu.SemaphoreType.DMA((slots,)),
                pltpu.SemaphoreType.DMA((len(inputs),)),
                pltpu.SemaphoreType.DMA((group,)),
            ]
            + ([pltpu.SemaphoreType.DMA] if turned is None else []),
        ),
        compiler_params=WIDE,
        cost_estimate=pl.CostEstimate(
            flops=2 * slots * count * (size * size * width + size * width * width),
            bytes_accessed=2 * slots * count * (size * size + width * width),
            transcendentals=0,
        ),
    )(order, cols, a_blocks, *inputs)


def member_sum(members, pool, row, k):
    total = pool[members[row, 0], k].astype(F32)
    for m in range(1, MEMBERS):
        total = total + pool[members[row, m], k].astype(F32)
    return total.astype(BF16)


def gather_kernel(first, count, sources, members, *refs):
    out, pool, held, sem, sem_out = refs[-5:]
    for copy in fill(refs[:sources], pool, sem):
        copy.wait()

    def one(row, carry):
        for k in range(count):
            held[row, k] = member_sum(members, pool, row, k)
        return carry

    lax.fori_loop(0, held.shape[0], one, 0, unroll=True)
    copy = pltpu.make_async_copy(held, out.at[:, pl.ds(first, count)], sem_out)
    copy.start()
    copy.wait()


def gather_rows(members, recv, so_far, shape, first, count):
    rows, _, width, _ = shape
    inputs = list(recv) + ([] if so_far is None else [so_far])
    slots = sum(part.shape[0] for part in recv)
    return pl.pallas_call(
        functools.partial(gather_kernel, first, count, len(recv)),
        out_shape=jax.ShapeDtypeStruct(shape, BF16),
        grid_spec=pltpu.PrefetchScalarGridSpec(
            num_scalar_prefetch=1,
            in_specs=[pl.BlockSpec(memory_space=ANY)] * len(inputs),
            out_specs=pl.BlockSpec(memory_space=ANY),
            scratch_shapes=[
                VMEM((slots, count, width, width), BF16),
                VMEM((rows, count, width, width), BF16),
                pltpu.SemaphoreType.DMA((len(recv),)),
                pltpu.SemaphoreType.DMA,
            ],
        ),
        input_output_aliases={} if so_far is None else {1 + len(recv): 0},
        compiler_params=pltpu.CompilerParams(vmem_limit_bytes=12 << 20),
        cost_estimate=pl.CostEstimate(
            flops=2 * slots * count * width * width,
            bytes_accessed=3 * slots * count * width * width,
            transcendentals=0,
        ),
    )(members, *inputs)


def block_row_product(blocks, pool, cols, row):
    total = None
    for k in range(0, len(blocks), 2):
        (left, at), lefts, rights = blocks[k], [], []
        for side in range(k, min(k + 2, len(blocks))):
            left, at = blocks[side]
            lefts.append(left[row, at])
            rights.append(pool[cols[row, side]])
        if len(lefts) > 1:
            term = dot(jnp.concatenate(lefts, axis=1), jnp.concatenate(rights, axis=0))
        else:
            term = dot(lefts[0], rights[0])
        total = term if total is None else total + term
    return total


def early_kernel(first, count, sources, members, cols, *refs):
    recv, refs = refs[:sources], refs[sources:]
    so_far, own, across, along, out, kept, product, scaled, sums, scale_out = refs[:10]
    slots, held, pool, sem, sem_in, sem_out = refs[10:]
    rows, width = product.shape[:2]
    copies = fill(recv, slots, sem)
    load = pltpu.make_async_copy(so_far.at[:, pl.ds(0, first)], held.at[:, pl.ds(0, first)], sem_in)
    load.start()
    for copy in copies:
        copy.wait()
    for row in range(rows):
        for k in range(count):
            held[row, first + k] = member_sum(members, slots, row, k)
    load.wait()
    stores = [
        pltpu.make_async_copy(
            held.at[:, pl.ds(first, count)], out.at[:, pl.ds(first, count)], sem_out.at[0]
        ),
        pltpu.make_async_copy(held, kept, sem_out.at[1]),
    ]
    for store in stores:
        store.start()
    most = jnp.zeros((width, 1), F32)
    for row in range(rows):
        total = jnp.abs(held[row, 0].astype(F32))
        for k in range(1, first + count):
            total = total + jnp.abs(held[row, k].astype(F32))
        sums[row] = total
        most = jnp.maximum(most, jnp.sum(total, axis=1, keepdims=True))
    held_scale = jnp.clip(jnp.max(most, axis=0, keepdims=True), 2.0**-100, 2.0**120)
    scale_out[...] = jnp.broadcast_to(held_scale, scale_out.shape)
    inverse = 1.0 / held_scale
    for part, source in enumerate((own, across, along)):
        for row in range(rows):
            pool[part * rows + row] = (source[row].astype(F32) * inverse).astype(BF16)
    stores.append(pltpu.make_async_copy(pool, scaled, sem_out.at[2]))
    stores[-1].start()
    blocks = [(held, k) for k in range(first + count)]
    for row in range(rows):
        product[row] = block_row_product(blocks, pool, cols, row)
    for store in stores:
        store.wait()


def early_product(members, cols, recv, so_far, own, across, along, first, count):
    rows, _, width, _ = so_far.shape
    vmem = pl.BlockSpec(memory_space=VMEM)
    hbm = pl.BlockSpec(memory_space=ANY)
    slots = sum(part.shape[0] for part in recv)
    held = (rows, first + count, width, width)
    pool = (3 * rows,) + own.shape[1:]
    return pl.pallas_call(
        functools.partial(early_kernel, first, count, len(recv)),
        out_shape=(
            jax.ShapeDtypeStruct(so_far.shape, BF16),
            jax.ShapeDtypeStruct(held, BF16),
            jax.ShapeDtypeStruct(own.shape, F32),
            jax.ShapeDtypeStruct(pool, BF16),
            jax.ShapeDtypeStruct((rows, width, width), F32),
            jax.ShapeDtypeStruct((8, 128), F32),
        ),
        grid_spec=pltpu.PrefetchScalarGridSpec(
            num_scalar_prefetch=2,
            in_specs=[hbm] * (len(recv) + 1) + [vmem] * 3,
            out_specs=(hbm, hbm, vmem, hbm, vmem, vmem),
            scratch_shapes=[
                VMEM((slots, count, width, width), BF16),
                VMEM(held, BF16),
                VMEM(pool, BF16),
                pltpu.SemaphoreType.DMA((len(recv),)),
                pltpu.SemaphoreType.DMA,
                pltpu.SemaphoreType.DMA((3,)),
            ],
        ),
        input_output_aliases={2 + len(recv): 0},
        compiler_params=pltpu.CompilerParams(vmem_limit_bytes=12 << 20),
        cost_estimate=pl.CostEstimate(
            flops=2 * so_far.size * own.shape[2],
            bytes_accessed=6 * so_far.size,
            transcendentals=0,
        ),
        name="early_product",
    )(members, cols, *recv, so_far, own, across, along)


def last_kernel(first, count, sources, members, cols, *refs):
    recv, refs = refs[:sources], refs[sources:]
    _, early, pool, sums, scale = refs[:5]
    out, kept, product, sent_a, sent_b, peak = refs[5:11]
    slots, held, sem, sem_out = refs[11:]
    rows, width = product.shape[:2]
    half = sent_a.shape[0]
    for copy in fill(recv, slots, sem):
        copy.wait()
    for row in range(rows):
        for k in range(count):
            held[row, k] = member_sum(members, slots, row, k)
    stores = [
        pltpu.make_async_copy(held, out.at[:, pl.ds(first, count)], sem_out.at[0]),
        pltpu.make_async_copy(held, kept, sem_out.at[1]),
    ]
    for store in stores:
        store.start()
    most = jnp.zeros((width, 1), F32)
    for row in range(rows):
        total = sums[row]
        for k in range(count):
            total = total + jnp.abs(held[row, k].astype(F32))
        most = jnp.maximum(most, jnp.sum(total, axis=1, keepdims=True))
    most = jnp.max(most, axis=0, keepdims=True)
    before = scale[0:1, 0:1]
    now = jnp.clip(most, 2.0**-100, 2.0**120)
    change = most > before * 2.0**60
    up = jnp.where(change, before, 1.0)
    down = jnp.where(change, 1.0 / now, 1.0)
    lane = lax.broadcasted_iota(jnp.int32, peak.shape[1:], 0)
    told = jnp.where(lane == 0, most, jnp.where(change, now, before))
    peak[...] = jnp.broadcast_to(told[None], peak.shape)
    for row in range(rows):
        total = early[row] * up * down
        for k in range(count):
            right = pool[cols[row, first + k]].astype(F32) * up * down
            total = total + dot(held[row, k], right.astype(BF16))
        product[row] = total
        if row < half:
            sent_a[row] = total.astype(BF16)
        else:
            sent_b[row - half] = total.astype(BF16)
    for store in stores:
        store.wait()


def last_product(members, cols, recv, so_far, early, pool, sums, scale, first, count, devices):
    rows, _, width, _ = so_far.shape
    half = (rows + 1) // 2
    vmem = pl.BlockSpec(memory_space=VMEM)
    hbm = pl.BlockSpec(memory_space=ANY)
    slots = sum(part.shape[0] for part in recv)
    held = (rows, count, width, width)
    return pl.pallas_call(
        functools.partial(last_kernel, first, count, len(recv)),
        out_shape=(
            jax.ShapeDtypeStruct(so_far.shape, BF16),
            jax.ShapeDtypeStruct(held, BF16),
            jax.ShapeDtypeStruct(early.shape, F32),
            pltpu.HBM((half,) + early.shape[1:], BF16),
            pltpu.HBM((rows - half,) + early.shape[1:], BF16),
            pltpu.HBM((devices, 8, 128), F32),
        ),
        grid_spec=pltpu.PrefetchScalarGridSpec(
            num_scalar_prefetch=2,
            in_specs=[hbm] * (len(recv) + 1) + [vmem] * 4,
            out_specs=(hbm, hbm, vmem, vmem, vmem, vmem),
            scratch_shapes=[
                VMEM((slots, count, width, width), BF16),
                VMEM(held, BF16),
                pltpu.SemaphoreType.DMA((len(recv),)),
                pltpu.SemaphoreType.DMA((2,)),
            ],
        ),
        input_output_aliases={2 + len(recv): 0},
        compiler_params=pltpu.CompilerParams(vmem_limit_bytes=30 << 20),
        cost_estimate=pl.CostEstimate(
            flops=2 * slots * count * width * early.shape[2],
            bytes_accessed=6 * early.size,
            transcendentals=0,
        ),
        name="last_product",
    )(members, cols, *[in_hbm(part) for part in recv], so_far, early, pool, sums, scale)


def second_kernel(
    cols, near, early, late, own, across, along, product,
    across_a, across_b, along_a, along_b, peaks, out, pool,
):
    rows = out.shape[0]
    half = across_a.shape[0]
    blocks = [(part, k) for part in (early, late) for k in range(part.shape[1])]
    largest = jnp.max(jnp.max(peaks[...], axis=0)[0:1], axis=1, keepdims=True)
    lower_end = largest / 30.0
    centre = (largest + lower_end) / 2.0
    half_width = (largest - lower_end) / 2.0
    sigma = centre / half_width
    weight_0 = 1.0 / sigma
    weight_1 = 1.0 / (2.0 * sigma - weight_0)
    weight_2 = 1.0 / (2.0 * sigma - weight_1)
    start = 1.0 / centre
    gain_1 = 2.0 * weight_1 / half_width
    gain_2 = 2.0 * weight_2 / half_width
    change = weight_1 * weight_0 * start + gain_1

    def back(slot):
        return gain_1 * (peaks[near[slot]][1:2, 0:1] / centre)

    pieces = (
        (0, 0, own, product),
        (1, 0, across, across_a),
        (1, half, across, across_b),
        (2, 0, along, along_a),
        (2, half, along, along_b),
    )
    for part, start_row, source, seen in pieces:
        factor = back(part)

        def iterate(row, carry):
            at = start_row + row
            value = (start + change) * source[at].astype(F32) - factor * seen[row].astype(F32)
            pool[part * rows + at] = value.astype(BF16)
            return carry

        lax.fori_loop(0, seen.shape[0], iterate, 0, unroll=True)
    mine = back(0)

    def multiply(row, carry):
        right = own[row].astype(F32)
        update = change * right - mine * product[row]
        residual = right - block_row_product(blocks, pool, cols, row)
        value = start * right + update + (weight_2 * weight_1 * update + gain_2 * residual)
        out[row] = value.astype(BF16)
        return carry

    lax.fori_loop(0, rows, multiply, 0, unroll=True)


def second_product(cols, near, kept, own, across, along, product, seen, peaks):
    rows = own.shape[0]
    vmem = pl.BlockSpec(memory_space=VMEM)
    return pl.pallas_call(
        second_kernel,
        out_shape=jax.ShapeDtypeStruct(own.shape, BF16),
        grid_spec=pltpu.PrefetchScalarGridSpec(
            num_scalar_prefetch=2,
            in_specs=[vmem] * 11,
            out_specs=vmem,
            scratch_shapes=[VMEM((3 * rows,) + own.shape[1:], BF16)],
        ),
        compiler_params=pltpu.CompilerParams(vmem_limit_bytes=50 << 20),
        cost_estimate=pl.CostEstimate(
            flops=2 * kept[0].size * own.shape[2],
            bytes_accessed=6 * kept[0].size,
            transcendentals=0,
        ),
        name="second_product",
    )(cols, near, *kept, own, across, along, product, *seen, peaks)


def exchange(block, axis):
    return lax.all_to_all(block, axis, split_axis=0, concat_axis=0, tiled=True)


def shifted(block, offset):
    count = lax.axis_size("gy")
    return lax.ppermute(block, "gy", [(i, (i + offset) % count) for i in range(count)])


def all_shifted(blocks):
    moved = []
    for offset, block in enumerate(blocks, 1):
        moved.append(shifted(block, offset))
    return moved


def to_partner(block):
    count = lax.axis_size("gy")
    return lax.ppermute(block, "gy", [(i, i ^ 1) for i in range(count) if i ^ 1 < count])


def pass_on(block):
    count = lax.axis_size("gy")
    steps = [(i, i + 2 if i % 2 == 0 else i - 2) for i in range(count)]
    return lax.ppermute(block, "gy", [(i, to) for i, to in steps if 0 <= to < count])


def past_partner(block):
    count = lax.axis_size("gy")
    steps = [(i, i - 2 if i % 2 == 0 else i + 2) for i in range(count)]
    return lax.ppermute(block, "gy", [(i, to) for i, to in steps if 0 <= to < count])


def to_other(block):
    count = lax.axis_size("gy")
    steps = [(i, i - 1 if i % 2 == 0 else i + 1) for i in range(count)]
    return lax.ppermute(block, "gy", [(i, to) for i, to in steps if 0 <= to < count])


def routes(fine_agg, balance, coarse_rows):
    group = lax.axis_size("gy")
    me = lax.axis_index("gy")
    rows = fine_agg.shape[0]
    facts = jnp.concatenate([fine_agg, balance.reshape(-1)])
    facts = exchange(jnp.broadcast_to(facts[None, None], (group, 1) + facts.shape), "gy")[:, 0]
    named, table = facts[:, :rows], facts[:, rows:].reshape(-1)
    keys = jnp.arange(table.shape[0], dtype=jnp.int32)
    target = jnp.sum(
        jnp.where(named[:, :, None] == keys[None, None, :], table[None, None, :], 0), axis=2
    )
    device = target // coarse_rows
    before = jnp.arange(rows)[:, None] > jnp.arange(rows)[None, :]
    rank = jnp.sum(
        ((device[:, :, None] == device[:, None, :]) & before[None]).astype(jnp.int32), axis=2
    )
    mine = (jnp.arange(group) == me)[:, None]
    place = jnp.sum(jnp.where(mine, (device - me) % group * OCAP + rank, 0), axis=0)
    slots = jnp.arange(group * OCAP, dtype=jnp.int32)
    order = jnp.sum(
        jnp.where(place[None, :] == slots[:, None], jnp.arange(rows, dtype=jnp.int32)[None, :], 0),
        axis=1,
    )
    goal = me * coarse_rows + jnp.arange(coarse_rows, dtype=jnp.int32)
    hit = target[None] == goal[:, None, None]
    slot = (me - jnp.arange(group, dtype=jnp.int32))[:, None] % group * OCAP + rank
    source = jnp.sum(jnp.where(hit, slot[None] + 1, 0), axis=2)
    found = (source > 0).astype(jnp.int32)
    earlier = jnp.arange(group)[:, None] < jnp.arange(group)[None, :]
    ordinal = jnp.sum(found[:, :, None] * earlier[None].astype(jnp.int32), axis=1)
    member = jnp.arange(MEMBERS, dtype=jnp.int32)[None, None, :]
    chosen = (ordinal[:, :, None] == member) & (found[:, :, None] > 0)
    members = jnp.sum(jnp.where(chosen, source[:, :, None] - 1, 0), axis=1)
    return order.astype(jnp.int32), members.astype(jnp.int32)


def step(a_blocks, prolong, neighbour, ghost_send, fine_agg, balance, coarse_cols, loads):
    block_rows, blocks = a_blocks.shape[:2]
    group = lax.axis_size("gy")
    row_gy = lax.axis_index("gy")
    row_gx = lax.axis_index("gx")
    devices = group * lax.axis_size("gx")
    coarse_rows = loads.shape[0]
    width = prolong.shape[2]
    cap = ghost_send.shape[3]

    beyond = past_partner(loads)
    picked = pick_ghosts(row_gy.astype(jnp.int32)[None], ghost_send[0, 0], prolong)
    arrived = all_shifted(picked)
    across = to_partner(loads)
    along = to_partner(beyond)
    order, members = routes(fine_agg, balance, coarse_rows)
    remote = neighbour - block_rows
    offset = (row_gy - remote // cap) % group
    neighbour = jnp.where(
        remote < 0, neighbour, block_rows + (offset - 1) * cap + remote % cap
    )
    columns = jnp.concatenate(
        [jnp.arange(block_rows, dtype=jnp.int32)[:, None], neighbour], axis=1
    )
    parts = chunks_of(blocks)
    received, turned = [], None
    for first, count in parts:
        sources = [prolong] + (arrived if first > 0 else [])
        sent = list(galerkin(a_blocks, sources, turned, order, columns, first, count))
        turned = sent.pop() if first == 0 else turned
        received.append(sent[:1] + all_shifted(sent[1:]))
    so_far = None
    for (first, count), recv in zip(parts[:-2], received[:-2]):
        shape = (coarse_rows, blocks, width, width)
        so_far = gather_rows(members, recv, so_far, shape, first, count)
    beside = coarse_cols // coarse_rows - (row_gx * group + row_gy)
    toward = 1 - 2 * (row_gy % 2)
    part = jnp.where(beside == 0, 0, jnp.where(beside == toward, 1, 2))
    local_cols = part * coarse_rows + coarse_cols % coarse_rows
    coarse, kept_early, early, pool, sums, scale = early_product(
        members, local_cols, received[-2], so_far, loads, across, along, *parts[-2]
    )
    coarse, kept_late, product, sent_a, sent_b, peak = last_product(
        members, local_cols, received[-1], coarse, early, pool, sums, scale, *parts[-1], devices
    )
    across_a = to_partner(sent_a)
    across_b = to_partner(sent_b)
    along_b = to_other(sent_b)
    along_a = pass_on(across_a)
    peaks = exchange(peak, ("gx", "gy"))
    here = row_gx * group + row_gy
    near = jnp.clip(jnp.stack([here, here + toward, here - toward]), 0, devices - 1)
    smoothed = second_product(
        local_cols,
        near.astype(jnp.int32),
        (kept_early, kept_late),
        loads,
        across,
        along,
        product,
        (across_a, across_b, along_a, along_b),
        peaks,
    )
    return coarse, smoothed


def solution(mesh):
    return jax.shard_map(
        step,
        mesh=mesh,
        in_specs=(
            P(("gx", "gy"), None, None, None),
            P(("gx", "gy"), None, None),
            P(("gx", "gy"), None),
            P("gx", "gy", None, None),
            P(("gx", "gy")),
            P("gx", "gy", None),
            P(("gx", "gy"), None),
            P(("gx", "gy"), None, None),
        ),
        out_specs=(P(("gx", "gy"), None, None, None), P(("gx", "gy"), None, None)),
        check_vma=False,
    )
```
